32 devices in a mesh: beam: 2 (over y), chan: 4 (over z), tgrp: 2 (over x), pol: 2 (over core).
Axes of the slice: x: 2, y: 2, z: 4, core: 2. Of those that a mesh axis runs over, the one named last changes fastest.
Arguments:
- voltages: bfloat16 [16, 8192, 512], P(('beam', 'chan', 'tgrp'), None, 'pol'), parts along dimension 0, may hold values from -6 to 6
- filter_taps: float32 [4, 8192], replicated, may hold values from -0.03125 to 0.03125
Outputs:
- visibility: float32 [512, 16, 2, 512], P('tgrp', ('beam', 'chan'), None, 'pol'), parts along dimension 1
The draws below stay inside these ranges and needn't reach their ends.
There are 2 independent parts, one for each index of `beam`. The reference program is written for one: setup_inputs(seed, part) draws one part's arguments, and reference() takes and returns one part's arrays. A program takes and returns all parts, laid end to end along the dimension named above; an argument that names none is the same for every part. Nothing has to cross between parts.
All inputs are finite; a program needn't handle non-finite values.
Results may differ from the reference program's by a relative error of at most 0.013.
Values may be sent and summed in bfloat16 or wider, within the bound.
A program may use at most 64 MiB of HBM per device.

```python
import jax
import jax.numpy as jnp
from jax import lax

LEN = 8192
INPUTS = 512
TAPS = 4
BAND_START = 1024
BAND = 8
FRAMES = 8


def block_scale(own_key, shape, cuts, least, largest):
    def one(position, shards_of):
        draws = jax.random.uniform(jax.random.fold_in(jax.random.fold_in(own_key, 6), position), (shards_of,), jnp.float32, least / len(cuts), largest / len(cuts))
        return jnp.repeat(jnp.exp(draws), shape[position] // shards_of).reshape((-1,) + (1,) * (len(shape) - position - 1))

    gain = one(*cuts[0])
    for cut in cuts[1:]:
        gain = gain * one(*cut)
    return gain


def centred(key, dims, width, bound, shards=(), held_as=jnp.bfloat16):
    result = width * jax.random.normal(key, dims, jnp.float32)
    if shards:
        result = result * block_scale(key, dims, shards, -0.22, 0.18)
    return jnp.clip(result, -bound, bound).astype(held_as)


def setup_inputs(seed: int = 0, part: int = 0) -> dict:
    key_of = jax.random.split(jax.random.key(seed), 3)
    part_splits = jax.random.split(jax.random.fold_in(key_of[2], part), 3)
    return {
        "voltages": centred(part_splits[0], (FRAMES, LEN, INPUTS), 1.0, 6.0, ((0, 8), (2, 2))),
        "filter_taps": centred(key_of[1], (TAPS, LEN), (TAPS * LEN) ** -0.5, 0.03125, (), jnp.float32),
    }


def reference(voltages, filter_taps):
    frames, length, inputs = voltages.shape
    lead_count = TAPS - 1

    def one_frame(frame_index):
        windowed = jnp.zeros((length, inputs), jnp.float32)
        for tap_index in range(TAPS):
            source = frame_index - lead_count + tap_index
            picked = lax.dynamic_index_in_dim(voltages, jnp.maximum(source, 0).astype(jnp.int32), 0, keepdims=False)
            weight = jnp.where(source >= 0, 1.0, 0.0).astype(jnp.float32)
            windowed = windowed + weight * filter_taps[tap_index][:, None] * picked.astype(jnp.float32)
        spectrum = jnp.fft.rfft(windowed, axis=0)[BAND_START:BAND_START + BAND]
        return jnp.stack([jnp.real(spectrum), jnp.imag(spectrum)], 0).astype(jnp.bfloat16)

    spectra = lax.map(one_frame, jnp.arange(frames, dtype=jnp.int32))
    wide_spectra = spectra.astype(jnp.float32)
    real_part = jnp.einsum("frki,frkj->ikj", wide_spectra, wide_spectra)
    imag_part = jnp.einsum("fki,fkj->ikj", wide_spectra[:, 1], wide_spectra[:, 0]) - jnp.einsum("fki,fkj->ikj", wide_spectra[:, 0], wide_spectra[:, 1])
    return jnp.stack([real_part, imag_part], 2) * (1.0 / FRAMES)
```

```python
import functools
import math

import jax
import jax.numpy as jnp
import numpy as np
from jax import lax
from jax.experimental import pallas as pl
from jax.experimental.pallas import tpu as pltpu
from jax.sharding import PartitionSpec as P

BAND_START = 1024
CH_DEV = 2
CHUNKS = 8
FUSED = False
LINK = jnp.bfloat16
MESH = pl.DeviceIdType.MESH


def twiddle_table(length, chans):
    block, part, sub = np.meshgrid(np.arange(chans), np.arange(2), np.arange(CH_DEV), indexing="ij")
    channel = (BAND_START + block * CH_DEV + sub).reshape(-1, 1)
    angles = (channel * np.arange(length)[None] % length) * (2.0 * math.pi / length)
    return np.where(part.reshape(-1, 1) == 0, np.cos(angles), -np.sin(angles)).astype(np.float32)


def tap_sum_matrix(frames, taps, swapped):
    rows, cols = CH_DEV * frames * 2, frames * taps * 2 * CH_DEV
    row = lax.broadcasted_iota(jnp.int32, (rows, cols), 0)
    col = lax.broadcasted_iota(jnp.int32, (rows, cols), 1)
    row_sub, row_frame, row_part = row // (2 * frames), row // 2 % frames, row % 2
    col_frame, col_tap = col // (taps * 2 * CH_DEV), col // (2 * CH_DEV) % taps
    col_part, col_sub = col // CH_DEV % 2, col % CH_DEV
    hit = (row_sub == col_sub) & (row_frame == col_frame + (taps - 1) - col_tap)
    if swapped:
        hit = hit & (row_part != col_part)
        value = jnp.where(row_part == 0, 1.0, -1.0)
    else:
        hit = hit & (row_part == col_part)
        value = jnp.float32(1.0)
    return jnp.where(hit, value, 0.0).astype(jnp.bfloat16)


def tap_summed(matrix, slots):
    flat = slots.reshape(slots.shape[0] * slots.shape[1], slots.shape[2])
    high = flat.astype(jnp.bfloat16)
    total = jnp.dot(matrix, high, preferred_element_type=jnp.float32)
    if flat.dtype == jnp.float32:
        low = (flat - high.astype(jnp.float32)).astype(jnp.bfloat16)
        total = total + jnp.dot(matrix, low, preferred_element_type=jnp.float32)
    return total.astype(jnp.bfloat16)


def cross_powers(out_ref, wide_ref, row_side, col_side, frames):
    half = col_side.shape[1]
    rows = out_ref.shape[0] * 128 // (CH_DEV * 2 * half)
    tiles = half // 128
    stride = CH_DEV * 2 * tiles
    for part in range(2):
        for sub in range(CH_DEV):
            span = slice(sub * 2 * frames, (sub + 1) * 2 * frames)
            vis = lax.dot_general(
                row_side[part][span],
                col_side[span],
                (((0,), (0,)), ((), ())),
                preferred_element_type=jnp.float32,
            ) * (1.0 / frames)
            if rows != half:
                wide_ref[...] = vis
                first = lax.axis_index("tgrp") * rows % half
                vis = wide_ref[pl.ds(pl.multiple_of(first, 8), rows), :]
            for tile in range(tiles):
                out_ref[pl.ds(sub * 2 * tiles + tile * 2 + part, rows, stride=stride), :] = vis[
                    :, tile * 128 : (tile + 1) * 128
                ]


def exchange_kernel(
    chans, groups, volt_hbm, taps_hbm, tw_hbm, rows_out, cols_out,
    volt, taps, tw, sent, cols, rows, load_sem, col_send, row_send, col_recv, row_recv,
):
    length, half = volt.shape
    tap_count = taps.shape[0]
    frames = chans * groups
    me_c, me_g, me_p = lax.axis_index("chan"), lax.axis_index("tgrp"), lax.axis_index("pol")
    me_f = me_c * groups + me_g
    per_half = groups // 2
    my_half = me_g // per_half
    chunk = length // CHUNKS

    loads = [
        pltpu.make_async_copy(taps_hbm, taps, load_sem.at[0]),
        pltpu.make_async_copy(tw_hbm, tw, load_sem.at[1]),
    ]
    for step in range(CHUNKS):
        span = pl.ds(step * chunk, chunk)
        loads.append(pltpu.make_async_copy(volt_hbm.at[0, span], volt.at[span], load_sem.at[2 + step]))
    for load in loads:
        load.start()

    barrier = pltpu.get_barrier_semaphore()
    for dc in range(chans):
        for dg in range(groups):
            for dp in range(2):
                if dc or dg or dp:
                    peer = {
                        "chan": lax.rem(me_c + dc, chans),
                        "tgrp": lax.rem(me_g + dg, groups),
                        "pol": lax.rem(me_p + dp, 2),
                    }
                    pl.semaphore_signal(barrier, inc=1, device_id=peer, device_id_type=MESH)

    matrix = tap_sum_matrix(frames, tap_count, False)
    swapped = tap_sum_matrix(frames, tap_count, True)

    loads[0].wait()
    loads[1].wait()
    band_rows = tw.shape[0]
    total = jnp.zeros((2 * tap_count * band_rows, half), jnp.float32)
    for step in range(CHUNKS):
        span = slice(step * chunk, (step + 1) * chunk)
        table = tw[:, span]
        wide = jnp.concatenate([table * taps[t : t + 1, span] for t in range(tap_count)], 0)
        high = wide.astype(jnp.bfloat16)
        low = (wide - high.astype(jnp.float32)).astype(jnp.bfloat16)
        loads[2 + step].wait()
        total = total + jnp.dot(
            jnp.concatenate([high, low], 0), volt[span], preferred_element_type=jnp.float32
        )
    terms = total[: tap_count * band_rows] + total[tap_count * band_rows :]
    per_block = 2 * CH_DEV
    for block in range(chans):
        sent[block] = jnp.concatenate(
            [
                terms[t * band_rows + block * per_block : t * band_rows + (block + 1) * per_block]
                for t in range(tap_count)
            ],
            0,
        ).astype(LINK)

    pl.semaphore_wait(barrier, chans * groups * 2 - 1)

    def col_copy(slot, to_c, to_g, index):
        return pltpu.make_async_remote_copy(
            src_ref=sent.at[to_c],
            dst_ref=cols.at[slot],
            send_sem=col_send.at[index],
            recv_sem=col_recv.at[slot],
            device_id={"chan": to_c, "tgrp": to_g, "pol": me_p},
            device_id_type=MESH,
        )

    def row_copy(slot, to_c, to_g, index):
        return pltpu.make_async_remote_copy(
            src_ref=sent.at[to_c],
            dst_ref=rows.at[slot],
            send_sem=row_send.at[index],
            recv_sem=row_recv.at[slot],
            device_id={"chan": to_c, "tgrp": to_g, "pol": 1 - me_p},
            device_id_type=MESH,
        )

    copies = []
    for dc in list(range(1, chans)) + [0]:
        to_c = lax.rem(me_c + dc, chans)
        for dg in range(groups):
            if dc or dg:
                copies.append(col_copy(me_f, to_c, lax.rem(me_g + dg, groups), dc * groups + dg))
                copies[-1].start()
        for member in range(per_half):
            to_g = me_p * per_half + member
            copies.append(row_copy(me_f, to_c, to_g, dc * per_half + member))
            copies[-1].start()
    cols[me_f] = sent[me_c]

    for dc in range(chans):
        for dg in range(groups):
            if dc or dg:
                from_c, from_g = lax.rem(me_c + dc, chans), lax.rem(me_g + dg, groups)
                col_copy(from_c * groups + from_g, me_c, me_g, 0).wait_recv()
    slots = cols[...]
    cols_out[...] = tap_summed(matrix, slots)

    @pl.when(my_half == me_p)
    def _():
        rows_out[0] = cols_out[...]
        rows_out[1] = tap_summed(swapped, slots)

    @pl.when(my_half != me_p)
    def _():
        for source in range(frames):
            row_copy(source, me_c, me_g, 0).wait_recv()
        far = rows[...]
        rows_out[0] = tap_summed(matrix, far)
        rows_out[1] = tap_summed(swapped, far)

    for copy in copies:
        copy.wait_send()


def power_kernel(frames, row_side, col_side, out_ref, *wide):
    cross_powers(out_ref, wide[0] if wide else None, row_side[...], col_side[...], frames)


def body(voltages, filter_taps):
    chans, groups = lax.axis_size("chan"), lax.axis_size("tgrp")
    _, length, half = voltages.shape
    taps = filter_taps.shape[0]
    frames = chans * groups
    slot = taps * 2 * CH_DEV
    table = jnp.asarray(twiddle_table(length, chans))
    vmem = pl.BlockSpec(memory_space=pltpu.VMEM)
    summed = CH_DEV * 2 * frames
    row_side, col_side = pl.pallas_call(
        functools.partial(exchange_kernel, chans, groups),
        out_shape=(
            jax.ShapeDtypeStruct((2, summed, half), jnp.bfloat16),
            jax.ShapeDtypeStruct((summed, half), jnp.bfloat16),
        ),
        in_specs=[pl.BlockSpec(memory_space=pl.ANY)] * 3,
        out_specs=(vmem, vmem),
        scratch_shapes=[
            pltpu.VMEM((length, half), jnp.bfloat16),
            pltpu.VMEM(filter_taps.shape, jnp.float32),
            pltpu.VMEM(table.shape, jnp.float32),
            pltpu.VMEM((chans, slot, half), LINK),
            pltpu.VMEM((frames, slot, half), LINK),
            pltpu.VMEM((frames, slot, half), LINK),
            pltpu.SemaphoreType.DMA((2 + CHUNKS,)),
            pltpu.SemaphoreType.DMA((frames,)),
            pltpu.SemaphoreType.DMA((frames // 2,)),
            pltpu.SemaphoreType.DMA((frames,)),
            pltpu.SemaphoreType.DMA((frames,)),
        ],
        compiler_params=pltpu.CompilerParams(collective_id=0, has_side_effects=True),
        name="exchange",
    )(voltages, filter_taps, table)
    rows = half * lax.axis_size("pol") // groups
    tiles = half // 128
    powers = pl.pallas_call(
        functools.partial(power_kernel, frames),
        out_shape=jax.ShapeDtypeStruct((rows * CH_DEV * tiles * 2, 128), jnp.float32),
        in_specs=[vmem, vmem],
        out_specs=vmem,
        scratch_shapes=[] if rows == half else [pltpu.VMEM((half, half), jnp.float32)],
        name="powers",
    )(row_side, col_side)
    powers = powers.reshape(rows, CH_DEV, tiles, 2, 128).transpose(0, 1, 3, 2, 4)
    return powers.reshape(rows, CH_DEV, 2, half)


def solution(mesh):
    return jax.shard_map(
        body,
        mesh=mesh,
        in_specs=(P(("beam", "chan", "tgrp"), None, "pol"), P()),
        out_specs=P("tgrp", ("beam", "chan"), None, "pol"),
        check_vma=False,
    )
```

```python
import functools
import math

import jax
import jax.numpy as jnp
import numpy as np
from jax import lax
from jax.experimental import pallas as pl
from jax.experimental.pallas import tpu as pltpu
from jax.sharding import PartitionSpec as P

BAND_START = 1024
CH_DEV = 2
CHUNKS = 8
VMEM_BYTES = 64 * 2**20
SPARE_BYTES = 72 * 2**10
LINK = jnp.bfloat16
MESH = pl.DeviceIdType.MESH


def twiddle_table(length, chans):
    block, part, sub = np.meshgrid(np.arange(chans), np.arange(2), np.arange(CH_DEV), indexing="ij")
    channel = (BAND_START + block * CH_DEV + sub).reshape(-1, 1)
    angles = (channel * np.arange(length)[None] % length) * (2.0 * math.pi / length)
    is_real = part.reshape(-1, 1) == 0
    chunk = length // CHUNKS
    near, turn = angles[:, :chunk], angles[:, ::chunk]
    table = np.zeros((2 * len(angles), chunk + 128), np.float32)
    table[: len(angles), :chunk] = np.where(is_real, np.cos(near), -np.sin(near))
    table[len(angles) :, :chunk] = np.where(is_real, -np.sin(near), np.cos(near))
    table[: len(angles), chunk : chunk + CHUNKS] = np.cos(turn)
    table[len(angles) :, chunk : chunk + CHUNKS] = np.where(is_real, np.sin(turn), -np.sin(turn))
    return table


def tap_sum_matrix(frames, taps, swapped):
    rows, cols = CH_DEV * frames * 2, frames * taps * 2 * CH_DEV
    row = lax.broadcasted_iota(jnp.int32, (rows, cols), 0)
    col = lax.broadcasted_iota(jnp.int32, (rows, cols), 1)
    row_sub, row_frame, row_part = row // (2 * frames), row // 2 % frames, row % 2
    col_frame, col_tap = col // (taps * 2 * CH_DEV), col // (2 * CH_DEV) % taps
    col_part, col_sub = col // CH_DEV % 2, col % CH_DEV
    hit = (row_sub == col_sub) & (row_frame == col_frame + (taps - 1) - col_tap)
    if swapped:
        hit = hit & (row_part != col_part)
        value = jnp.where(row_part == 0, 1.0, -1.0)
    else:
        hit = hit & (row_part == col_part)
        value = jnp.float32(1.0)
    return jnp.where(hit, value, 0.0).astype(jnp.bfloat16)


def tap_summed(matrix, slots):
    flat = slots.reshape(slots.shape[0] * slots.shape[1], slots.shape[2])
    high = flat.astype(jnp.bfloat16)
    total = jnp.dot(matrix, high, preferred_element_type=jnp.float32)
    if flat.dtype == jnp.float32:
        low = (flat - high.astype(jnp.float32)).astype(jnp.bfloat16)
        total = total + jnp.dot(matrix, low, preferred_element_type=jnp.float32)
    return total.astype(jnp.bfloat16)


def power_kernel(frames, row_side, col_side, out_hbm, out_ref, wide_ref, sems):
    half = col_side.shape[1]
    rows = out_ref.shape[0] * 128 // (CH_DEV * 2 * half)
    tiles = half // 128
    stride = CH_DEV * 2 * tiles
    pieces = rows // 128 if rows == half else 1
    size = rows // pieces
    writes = []
    for piece in range(pieces):
        for part in range(2):
            for sub in range(CH_DEV):
                span = slice(sub * 2 * frames, (sub + 1) * 2 * frames)
                lanes = slice(piece * size, (piece + 1) * size) if rows == half else slice(None)
                vis = lax.dot_general(
                    row_side[part, span, lanes],
                    col_side[span],
                    (((0,), (0,)), ((), ())),
                    preferred_element_type=jnp.float32,
                ) * (1.0 / frames)
                if rows != half:
                    wide_ref[...] = vis
                    first = lax.axis_index("tgrp") * rows % half
                    vis = wide_ref[pl.ds(pl.multiple_of(first, 8), rows), :]
                for tile in range(tiles):
                    start = piece * size * stride + sub * 2 * tiles + tile * 2 + part
                    out_ref[pl.ds(start, size, stride=stride), :] = vis[:, tile * 128 : (tile + 1) * 128]
        region = pl.ds(piece * size * stride, size * stride)
        writes.append(pltpu.make_async_copy(out_ref.at[region], out_hbm.at[region], sems.at[piece]))
        writes[-1].start()
    for write in writes:
        write.wait()


def exchange_kernel(
    chans, groups, volt_hbm, taps_hbm, tw_hbm, rows_out, cols_out,
    volt, taps, tw, sent, cols, rows, load_sem, col_send, row_send, col_recv, row_recv,
):
    length, half = volt.shape
    tap_count = taps.shape[0]
    frames = chans * groups
    me_c, me_g, me_p = lax.axis_index("chan"), lax.axis_index("tgrp"), lax.axis_index("pol")
    me_f = me_c * groups + me_g
    per_half = groups // 2
    my_half = me_g // per_half
    chunk = length // CHUNKS

    loads = [
        pltpu.make_async_copy(taps_hbm, taps, load_sem.at[0]),
        pltpu.make_async_copy(tw_hbm, tw, load_sem.at[1]),
    ]
    for step in range(CHUNKS):
        span = pl.ds(step * chunk, chunk)
        loads.append(pltpu.make_async_copy(volt_hbm.at[0, span], volt.at[span], load_sem.at[2 + step]))
    for load in loads:
        load.start()

    barrier = pltpu.get_barrier_semaphore()
    for dc in range(chans):
        for dg in range(groups):
            for dp in range(2):
                if dc or dg or dp:
                    peer = {
                        "chan": lax.rem(me_c + dc, chans),
                        "tgrp": lax.rem(me_g + dg, groups),
                        "pol": lax.rem(me_p + dp, 2),
                    }
                    pl.semaphore_signal(barrier, inc=1, device_id=peer, device_id_type=MESH)

    matrix = tap_sum_matrix(frames, tap_count, False)
    swapped = tap_sum_matrix(frames, tap_count, True)

    loads[0].wait()
    loads[1].wait()
    band_rows = tw.shape[0] // 2
    own, other = tw[:band_rows, :chunk], tw[band_rows:, :chunk]
    total = jnp.zeros((2 * tap_count * band_rows, half), jnp.float32)
    for step in range(CHUNKS):
        span = slice(step * chunk, (step + 1) * chunk)
        column = slice(chunk + step, chunk + step + 1)
        table = tw[:band_rows, column] * own + tw[band_rows:, column] * other
        wide = jnp.concatenate([table * taps[t : t + 1, span] for t in range(tap_count)], 0)
        high = wide.astype(jnp.bfloat16)
        low = (wide - high.astype(jnp.float32)).astype(jnp.bfloat16)
        loads[2 + step].wait()
        total = total + jnp.dot(
            jnp.concatenate([high, low], 0), volt[span], preferred_element_type=jnp.float32
        )
    terms = total[: tap_count * band_rows] + total[tap_count * band_rows :]
    per_block = 2 * CH_DEV
    for block in range(chans):
        sent[block] = jnp.concatenate(
            [
                terms[t * band_rows + block * per_block : t * band_rows + (block + 1) * per_block]
                for t in range(tap_count)
            ],
            0,
        ).astype(LINK)

    pl.semaphore_wait(barrier, chans * groups * 2 - 1)

    def col_copy(slot, to_c, to_g, index):
        return pltpu.make_async_remote_copy(
            src_ref=sent.at[to_c],
            dst_ref=cols.at[slot],
            send_sem=col_send.at[index],
            recv_sem=col_recv.at[slot],
            device_id={"chan": to_c, "tgrp": to_g, "pol": me_p},
            device_id_type=MESH,
        )

    def row_copy(slot, to_c, to_g, index):
        return pltpu.make_async_remote_copy(
            src_ref=sent.at[to_c],
            dst_ref=rows.at[slot],
            send_sem=row_send.at[index],
            recv_sem=row_recv.at[slot],
            device_id={"chan": to_c, "tgrp": to_g, "pol": 1 - me_p},
            device_id_type=MESH,
        )

    def each_send(act):
        for place in range(chans):
            to_c = jnp.where(me_c < chans // 2, chans - 1 - place, place)
            for dg in reversed(range(groups)):
                to_g = lax.rem(me_g + dg, groups)
                copy = col_copy(me_f, to_c, to_g, place * groups + dg)
                if dg:
                    act(copy)
                else:
                    pl.when(to_c != me_c)(functools.partial(act, copy))
            for member in range(per_half):
                act(row_copy(me_f, to_c, me_p * per_half + member, place * per_half + member))

    each_send(lambda copy: copy.start())
    cols[me_f] = sent[me_c]

    for dc in range(chans):
        for dg in range(groups):
            if dc or dg:
                from_c, from_g = lax.rem(me_c + dc, chans), lax.rem(me_g + dg, groups)
                col_copy(from_c * groups + from_g, me_c, me_g, 0).wait_recv()
    slots = cols[...]
    cols_out[...] = tap_summed(matrix, slots)

    @pl.when(my_half == me_p)
    def _():
        rows_out[0] = cols_out[...]
        rows_out[1] = tap_summed(swapped, slots)

    @pl.when(my_half != me_p)
    def _():
        for source in range(frames):
            row_copy(source, me_c, me_g, 0).wait_recv()
        far = rows[...]
        rows_out[0] = tap_summed(matrix, far)
        rows_out[1] = tap_summed(swapped, far)

    each_send(lambda copy: copy.wait_send())


def body(voltages, filter_taps):
    chans, groups = lax.axis_size("chan"), lax.axis_size("tgrp")
    _, length, half = voltages.shape
    taps = filter_taps.shape[0]
    frames = chans * groups
    slot = taps * 2 * CH_DEV
    table = jnp.asarray(twiddle_table(length, chans))
    vmem = pl.BlockSpec(memory_space=pltpu.VMEM)
    summed = CH_DEV * 2 * frames
    row_side, col_side = pl.pallas_call(
        functools.partial(exchange_kernel, chans, groups),
        out_shape=(
            pltpu.VMEM((2, summed, half), jnp.bfloat16),
            pltpu.VMEM((summed, half), jnp.bfloat16),
        ),
        in_specs=[pl.BlockSpec(memory_space=pl.ANY)] * 3,
        out_specs=(vmem, vmem),
        scratch_shapes=[
            pltpu.VMEM((length, half), jnp.bfloat16),
            pltpu.VMEM(filter_taps.shape, jnp.float32),
            pltpu.VMEM(table.shape, jnp.float32),
            pltpu.VMEM((chans, slot, half), LINK),
            pltpu.VMEM((frames, slot, half), LINK),
            pltpu.VMEM((frames, slot, half), LINK),
            pltpu.SemaphoreType.DMA((2 + CHUNKS,)),
            pltpu.SemaphoreType.DMA((frames,)),
            pltpu.SemaphoreType.DMA((frames // 2,)),
            pltpu.SemaphoreType.DMA((frames,)),
            pltpu.SemaphoreType.DMA((frames,)),
        ],
        compiler_params=pltpu.CompilerParams(collective_id=0, has_side_effects=True, vmem_limit_bytes=VMEM_BYTES - SPARE_BYTES - 6 * summed * half),
        name="exchange",
    )(voltages, filter_taps, table)
    rows = half * lax.axis_size("pol") // groups
    tiles = half // 128
    powers = pl.pallas_call(
        functools.partial(power_kernel, frames),
        out_shape=jax.ShapeDtypeStruct((rows * CH_DEV * tiles * 2, 128), jnp.float32),
        in_specs=[vmem, vmem],
        out_specs=pl.BlockSpec(memory_space=pltpu.HBM),
        scratch_shapes=[
            pltpu.VMEM((rows * CH_DEV * tiles * 2, 128), jnp.float32),
            pltpu.VMEM((half, half) if rows != half else (8, 128), jnp.float32),
            pltpu.SemaphoreType.DMA((max(1, rows // 128),)),
        ],
        compiler_params=pltpu.CompilerParams(vmem_limit_bytes=VMEM_BYTES // 4),
        name="powers",
    )(row_side, col_side)
    powers = powers.reshape(rows, CH_DEV, tiles, 2, 128).transpose(0, 1, 3, 2, 4)
    return powers.reshape(rows, CH_DEV, 2, half)


def solution(mesh):
    return jax.shard_map(
        body,
        mesh=mesh,
        in_specs=(P(("beam", "chan", "tgrp"), None, "pol"), P()),
        out_specs=P("tgrp", ("beam", "chan"), None, "pol"),
        check_vma=False,
    )
```

```python
import functools
import math

import jax
import jax.numpy as jnp
import numpy as np
from jax import lax
from jax.experimental import pallas as pl
from jax.experimental.pallas import tpu as pltpu
from jax.sharding import PartitionSpec as P

BAND_START = 1024
CH_DEV = 2
CHUNKS = 8
VMEM_BYTES = 64 * 2**20
SPARE_BYTES = 72 * 2**10
LINK = jnp.bfloat16
MESH = pl.DeviceIdType.MESH


def twiddle_table(length, chans):
    block, part, sub = np.meshgrid(np.arange(chans), np.arange(2), np.arange(CH_DEV), indexing="ij")
    channel = (BAND_START + block * CH_DEV + sub).reshape(-1, 1)
    angles = (channel * np.arange(length)[None] % length) * (2.0 * math.pi / length)
    is_real = part.reshape(-1, 1) == 0
    chunk = length // CHUNKS
    near, turn = angles[:, :chunk], angles[:, ::chunk]
    table = np.zeros((2 * len(angles), chunk + 128), np.float32)
    table[: len(angles), :chunk] = np.where(is_real, np.cos(near), -np.sin(near))
    table[len(angles) :, :chunk] = np.where(is_real, -np.sin(near), np.cos(near))
    table[: len(angles), chunk : chunk + CHUNKS] = np.cos(turn)
    table[len(angles) :, chunk : chunk + CHUNKS] = np.where(is_real, np.sin(turn), -np.sin(turn))
    return table


def tap_sum_matrix(frames, taps, swapped):
    rows, cols = CH_DEV * frames * 2, frames * taps * 2 * CH_DEV
    row = lax.broadcasted_iota(jnp.int32, (rows, cols), 0)
    col = lax.broadcasted_iota(jnp.int32, (rows, cols), 1)
    row_sub, row_frame, row_part = row // (2 * frames), row // 2 % frames, row % 2
    col_frame, col_tap = col // (taps * 2 * CH_DEV), col // (2 * CH_DEV) % taps
    col_part, col_sub = col // CH_DEV % 2, col % CH_DEV
    hit = (row_sub == col_sub) & (row_frame == col_frame + (taps - 1) - col_tap)
    if swapped:
        hit = hit & (row_part != col_part)
        value = jnp.where(row_part == 0, 1.0, -1.0)
    else:
        hit = hit & (row_part == col_part)
        value = jnp.float32(1.0)
    return jnp.where(hit, value, 0.0).astype(jnp.bfloat16)


def tap_summed(matrix, slots):
    flat = slots.reshape(slots.shape[0] * slots.shape[1], slots.shape[2])
    high = flat.astype(jnp.bfloat16)
    total = jnp.dot(matrix, high, preferred_element_type=jnp.float32)
    if flat.dtype == jnp.float32:
        low = (flat - high.astype(jnp.float32)).astype(jnp.bfloat16)
        total = total + jnp.dot(matrix, low, preferred_element_type=jnp.float32)
    return total.astype(jnp.bfloat16)


def power_kernel(frames, row_side, col_side, out_hbm, out_ref, wide_ref, sems):
    half = col_side.shape[1]
    rows = out_ref.shape[0] * 128 // (CH_DEV * 2 * half)
    tiles = half // 128
    stride = CH_DEV * 2 * tiles
    pieces = rows // 128 if rows == half else 1
    size = rows // pieces
    writes = []
    for piece in range(pieces):
        for part in range(2):
            for sub in range(CH_DEV):
                span = slice(sub * 2 * frames, (sub + 1) * 2 * frames)
                lanes = slice(piece * size, (piece + 1) * size) if rows == half else slice(None)
                vis = lax.dot_general(
                    row_side[part, span, lanes],
                    col_side[span],
                    (((0,), (0,)), ((), ())),
                    preferred_element_type=jnp.float32,
                ) * (1.0 / frames)
                if rows != half:
                    wide_ref[...] = vis
                    first = lax.axis_index("tgrp") * rows % half
                    vis = wide_ref[pl.ds(pl.multiple_of(first, 8), rows), :]
                for tile in range(tiles):
                    start = piece * size * stride + sub * 2 * tiles + tile * 2 + part
                    out_ref[pl.ds(start, size, stride=stride), :] = vis[:, tile * 128 : (tile + 1) * 128]
        region = pl.ds(piece * size * stride, size * stride)
        writes.append(pltpu.make_async_copy(out_ref.at[region], out_hbm.at[region], sems.at[piece]))
        writes[-1].start()
    for write in writes:
        write.wait()


def exchange_kernel(
    chans, groups, volt_hbm, taps_hbm, tw_hbm, rows_out, cols_out,
    volt, taps, tw, sent, cols, rows, load_sem, col_send, row_send, col_recv, row_recv,
):
    length, half = volt.shape
    tap_count = taps.shape[0]
    frames = chans * groups
    me_c, me_g, me_p = lax.axis_index("chan"), lax.axis_index("tgrp"), lax.axis_index("pol")
    me_f = me_c * groups + me_g
    per_half = groups // 2
    my_half = me_g // per_half
    chunk = length // CHUNKS
    per_block = 2 * CH_DEV

    loads = [
        pltpu.make_async_copy(taps_hbm, taps, load_sem.at[0]),
        pltpu.make_async_copy(tw_hbm, tw, load_sem.at[1]),
    ]
    for step in range(CHUNKS):
        span = pl.ds(step * chunk, chunk)
        loads.append(pltpu.make_async_copy(volt_hbm.at[0, span], volt.at[span], load_sem.at[2 + step]))
    for load in loads:
        load.start()

    barrier = pltpu.get_barrier_semaphore()
    for dc in range(chans):
        for dg in range(groups):
            for dp in range(2):
                if dc or dg or dp:
                    peer = {
                        "chan": lax.rem(me_c + dc, chans),
                        "tgrp": lax.rem(me_g + dg, groups),
                        "pol": lax.rem(me_p + dp, 2),
                    }
                    pl.semaphore_signal(barrier, inc=1, device_id=peer, device_id_type=MESH)

    matrix = tap_sum_matrix(frames, tap_count, False)
    both = jnp.concatenate([matrix, tap_sum_matrix(frames, tap_count, True)], 0)

    loads[0].wait()
    loads[1].wait()
    band_rows = tw.shape[0] // 2
    own, other = tw[:band_rows, :chunk], tw[band_rows:, :chunk]
    total = jnp.zeros((2 * tap_count * band_rows, half), jnp.float32)
    for step in range(CHUNKS):
        span = slice(step * chunk, (step + 1) * chunk)
        column = slice(chunk + step, chunk + step + 1)
        table = tw[:band_rows, column] * own + tw[band_rows:, column] * other
        gains = jnp.concatenate(
            [jnp.broadcast_to(taps[t : t + 1, span], (per_block, chunk)) for t in range(tap_count)], 0
        )
        wide = jnp.concatenate(
            [
                jnp.concatenate([table[b * per_block : (b + 1) * per_block]] * tap_count, 0) * gains
                for b in range(chans)
            ],
            0,
        )
        high = wide.astype(jnp.bfloat16)
        low = (wide - high.astype(jnp.float32)).astype(jnp.bfloat16)
        loads[2 + step].wait()
        total = total + jnp.dot(
            jnp.concatenate([high, low], 0), volt[span], preferred_element_type=jnp.float32
        )
    terms = total[: tap_count * band_rows] + total[tap_count * band_rows :]
    sent[...] = terms.reshape(sent.shape).astype(LINK)

    pl.semaphore_wait(barrier, chans * groups * 2 - 1)

    def col_copy(slot, to_c, to_g, index):
        return pltpu.make_async_remote_copy(
            src_ref=sent.at[to_c],
            dst_ref=cols.at[slot],
            send_sem=col_send.at[index],
            recv_sem=col_recv.at[slot],
            device_id={"chan": to_c, "tgrp": to_g, "pol": me_p},
            device_id_type=MESH,
        )

    def row_copy(slot, to_c, to_g, index):
        return pltpu.make_async_remote_copy(
            src_ref=sent.at[to_c],
            dst_ref=rows.at[slot],
            send_sem=row_send.at[index],
            recv_sem=row_recv.at[slot],
            device_id={"chan": to_c, "tgrp": to_g, "pol": 1 - me_p},
            device_id_type=MESH,
        )

    def each_send(act):
        for place in range(chans):
            to_c = jnp.where(me_c < chans // 2, chans - 1 - place, place)
            for dg in reversed(range(groups)):
                to_g = lax.rem(me_g + dg, groups)
                copy = col_copy(me_f, to_c, to_g, place * groups + dg)
                if dg:
                    act(copy)
                else:
                    pl.when(to_c != me_c)(functools.partial(act, copy))
            for member in range(per_half):
                act(row_copy(me_f, to_c, me_p * per_half + member, place * per_half + member))

    each_send(lambda copy: copy.start())
    cols[me_f] = sent[me_c]

    for dc in range(chans):
        for dg in range(groups):
            if dc or dg:
                from_c, from_g = lax.rem(me_c + dc, chans), lax.rem(me_g + dg, groups)
                col_copy(from_c * groups + from_g, me_c, me_g, 0).wait_recv()
    def put_rows(summed):
        rows_out[0] = summed[: matrix.shape[0]]
        rows_out[1] = summed[matrix.shape[0] :]

    @pl.when(my_half == me_p)
    def _():
        summed = tap_summed(both, cols[...])
        cols_out[...] = summed[: matrix.shape[0]]
        put_rows(summed)

    @pl.when(my_half != me_p)
    def _():
        cols_out[...] = tap_summed(matrix, cols[...])
        for source in range(frames):
            row_copy(source, me_c, me_g, 0).wait_recv()
        put_rows(tap_summed(both, rows[...]))

    each_send(lambda copy: copy.wait_send())


def body(voltages, filter_taps):
    chans, groups = lax.axis_size("chan"), lax.axis_size("tgrp")
    _, length, half = voltages.shape
    taps = filter_taps.shape[0]
    frames = chans * groups
    slot = taps * 2 * CH_DEV
    table = jnp.asarray(twiddle_table(length, chans))
    vmem = pl.BlockSpec(memory_space=pltpu.VMEM)
    summed = CH_DEV * 2 * frames
    row_side, col_side = pl.pallas_call(
        functools.partial(exchange_kernel, chans, groups),
        out_shape=(
            pltpu.VMEM((2, summed, half), jnp.bfloat16),
            pltpu.VMEM((summed, half), jnp.bfloat16),
        ),
        in_specs=[pl.BlockSpec(memory_space=pl.ANY)] * 3,
        out_specs=(vmem, vmem),
        scratch_shapes=[
            pltpu.VMEM((length, half), jnp.bfloat16),
            pltpu.VMEM(filter_taps.shape, jnp.float32),
            pltpu.VMEM(table.shape, jnp.float32),
            pltpu.VMEM((chans, slot, half), LINK),
            pltpu.VMEM((frames, slot, half), LINK),
            pltpu.VMEM((frames, slot, half), LINK),
            pltpu.SemaphoreType.DMA((2 + CHUNKS,)),
            pltpu.SemaphoreType.DMA((frames,)),
            pltpu.SemaphoreType.DMA((frames // 2,)),
            pltpu.SemaphoreType.DMA((frames,)),
            pltpu.SemaphoreType.DMA((frames,)),
        ],
        compiler_params=pltpu.CompilerParams(collective_id=0, has_side_effects=True, vmem_limit_bytes=VMEM_BYTES - SPARE_BYTES - 6 * summed * half),
        name="exchange",
    )(voltages, filter_taps, table)
    rows = half * lax.axis_size("pol") // groups
    tiles = half // 128
    powers = pl.pallas_call(
        functools.partial(power_kernel, frames),
        out_shape=jax.ShapeDtypeStruct((rows * CH_DEV * tiles * 2, 128), jnp.float32),
        in_specs=[vmem, vmem],
        out_specs=pl.BlockSpec(memory_space=pltpu.HBM),
        scratch_shapes=[
            pltpu.VMEM((rows * CH_DEV * tiles * 2, 128), jnp.float32),
            pltpu.VMEM((half, half) if rows != half else (8, 128), jnp.float32),
            pltpu.SemaphoreType.DMA((max(1, rows // 128),)),
        ],
        compiler_params=pltpu.CompilerParams(vmem_limit_bytes=VMEM_BYTES // 4),
        name="powers",
    )(row_side, col_side)
    powers = powers.reshape(rows, CH_DEV, tiles, 2, 128).transpose(0, 1, 3, 2, 4)
    return powers.reshape(rows, CH_DEV, 2, half)


def solution(mesh):
    return jax.shard_map(
        body,
        mesh=mesh,
        in_specs=(P(("beam", "chan", "tgrp"), None, "pol"), P()),
        out_specs=P("tgrp", ("beam", "chan"), None, "pol"),
        check_vma=False,
    )
```

```python
import functools
import math

import jax
import jax.numpy as jnp
import numpy as np
from jax import lax
from jax.experimental import pallas as pl
from jax.experimental.pallas import tpu as pltpu
from jax.sharding import PartitionSpec as P

BAND_START = 1024
CH_DEV = 2
CHUNKS = 8
VMEM_BYTES = 64 * 2**20
SPARE_BYTES = 72 * 2**10
LINK = jnp.bfloat16
MESH = pl.DeviceIdType.MESH


def twiddle_table(length, chans):
    block, part, sub = np.meshgrid(np.arange(chans), np.arange(2), np.arange(CH_DEV), indexing="ij")
    channel = (BAND_START + block * CH_DEV + sub).reshape(-1, 1)
    angles = (channel * np.arange(length)[None] % length) * (2.0 * math.pi / length)
    is_real = part.reshape(-1, 1) == 0
    chunk = length // CHUNKS
    near, turn = angles[:, :chunk], angles[:, ::chunk]
    table = np.zeros((2 * len(angles), chunk + 128), np.float32)
    table[: len(angles), :chunk] = np.where(is_real, np.cos(near), -np.sin(near))
    table[len(angles) :, :chunk] = np.where(is_real, -np.sin(near), np.cos(near))
    table[: len(angles), chunk : chunk + CHUNKS] = np.cos(turn)
    table[len(angles) :, chunk : chunk + CHUNKS] = np.where(is_real, np.sin(turn), -np.sin(turn))
    return table


def tap_sum_matrix(frames, taps, swapped):
    rows, cols = CH_DEV * frames * 2, frames * taps * 2 * CH_DEV
    row = lax.broadcasted_iota(jnp.int32, (rows, cols), 0)
    col = lax.broadcasted_iota(jnp.int32, (rows, cols), 1)
    row_sub, row_frame, row_part = row // (2 * frames), row // 2 % frames, row % 2
    col_frame, col_tap = col // (taps * 2 * CH_DEV), col // (2 * CH_DEV) % taps
    col_part, col_sub = col // CH_DEV % 2, col % CH_DEV
    hit = (row_sub == col_sub) & (row_frame == col_frame + (taps - 1) - col_tap)
    if swapped:
        hit = hit & (row_part != col_part)
        value = jnp.where(row_part == 0, 1.0, -1.0)
    else:
        hit = hit & (row_part == col_part)
        value = jnp.float32(1.0)
    return jnp.where(hit, value, 0.0).astype(jnp.bfloat16)


def tap_summed(matrix, slots):
    flat = slots.reshape(slots.shape[0] * slots.shape[1], slots.shape[2])
    high = flat.astype(jnp.bfloat16)
    total = jnp.dot(matrix, high, preferred_element_type=jnp.float32)
    if flat.dtype == jnp.float32:
        low = (flat - high.astype(jnp.float32)).astype(jnp.bfloat16)
        total = total + jnp.dot(matrix, low, preferred_element_type=jnp.float32)
    return total.astype(jnp.bfloat16)


def power_kernel(frames, row_side, col_side, out_hbm, out_ref, wide_ref, sems):
    half = col_side.shape[1]
    rows = out_ref.shape[0] * 128 // (CH_DEV * 2 * half)
    tiles = half // 128
    stride = CH_DEV * 2 * tiles
    pieces = rows // 64 if rows == half else 1
    size = rows // pieces
    writes = []
    for piece in range(pieces):
        for part in range(2):
            for sub in range(CH_DEV):
                span = slice(sub * 2 * frames, (sub + 1) * 2 * frames)
                lanes = slice(piece * size, (piece + 1) * size) if rows == half else slice(None)
                vis = lax.dot_general(
                    row_side[part, span, lanes],
                    col_side[span],
                    (((0,), (0,)), ((), ())),
                    preferred_element_type=jnp.float32,
                ) * (1.0 / frames)
                if rows != half:
                    wide_ref[...] = vis
                    first = lax.axis_index("tgrp") * rows % half
                    vis = wide_ref[pl.ds(pl.multiple_of(first, 8), rows), :]
                for tile in range(tiles):
                    start = piece * size * stride + sub * 2 * tiles + tile * 2 + part
                    out_ref[pl.ds(start, size, stride=stride), :] = vis[:, tile * 128 : (tile + 1) * 128]
        region = pl.ds(piece * size * stride, size * stride)
        writes.append(pltpu.make_async_copy(out_ref.at[region], out_hbm.at[region], sems.at[piece]))
        writes[-1].start()
    for write in writes:
        write.wait()


def exchange_kernel(
    chans, groups, volt_hbm, taps_hbm, tw_hbm, rows_out, cols_out,
    volt, taps, tw, sent, cols, rows, load_sem, col_send, row_send, col_recv, row_recv,
):
    length, half = volt.shape
    tap_count = taps.shape[0]
    frames = chans * groups
    me_c, me_g, me_p = lax.axis_index("chan"), lax.axis_index("tgrp"), lax.axis_index("pol")
    me_f = me_c * groups + me_g
    per_half = groups // 2
    my_half = me_g // per_half
    chunk = length // CHUNKS
    per_block = 2 * CH_DEV

    loads = [
        pltpu.make_async_copy(taps_hbm, taps, load_sem.at[0]),
        pltpu.make_async_copy(tw_hbm, tw, load_sem.at[1]),
    ]
    for step in range(CHUNKS):
        span = pl.ds(step * chunk, chunk)
        loads.append(pltpu.make_async_copy(volt_hbm.at[0, span], volt.at[span], load_sem.at[2 + step]))
    for load in loads:
        load.start()

    barrier = pltpu.get_barrier_semaphore()
    for dc in range(chans):
        for dg in range(groups):
            for dp in range(2):
                if dc or dg or dp:
                    peer = {
                        "chan": lax.rem(me_c + dc, chans),
                        "tgrp": lax.rem(me_g + dg, groups),
                        "pol": lax.rem(me_p + dp, 2),
                    }
                    pl.semaphore_signal(barrier, inc=1, device_id=peer, device_id_type=MESH)

    matrix = tap_sum_matrix(frames, tap_count, False)
    both = jnp.concatenate([matrix, tap_sum_matrix(frames, tap_count, True)], 0)

    loads[0].wait()
    loads[1].wait()
    band_rows = tw.shape[0] // 2
    own, other = tw[:band_rows, :chunk], tw[band_rows:, :chunk]
    total = jnp.zeros((2 * tap_count * band_rows, half), jnp.float32)
    for step in range(CHUNKS):
        span = slice(step * chunk, (step + 1) * chunk)
        column = slice(chunk + step, chunk + step + 1)
        table = tw[:band_rows, column] * own + tw[band_rows:, column] * other
        gains = jnp.concatenate(
            [jnp.broadcast_to(taps[t : t + 1, span], (per_block, chunk)) for t in range(tap_count)], 0
        )
        wide = jnp.concatenate(
            [
                jnp.concatenate([table[b * per_block : (b + 1) * per_block]] * tap_count, 0) * gains
                for b in range(chans)
            ],
            0,
        )
        high = wide.astype(jnp.bfloat16)
        low = (wide - high.astype(jnp.float32)).astype(jnp.bfloat16)
        loads[2 + step].wait()
        total = total + jnp.dot(
            jnp.concatenate([high, low], 0), volt[span], preferred_element_type=jnp.float32
        )
    terms = total[: tap_count * band_rows] + total[tap_count * band_rows :]
    sent[...] = terms.reshape(sent.shape).astype(LINK)

    pl.semaphore_wait(barrier, chans * groups * 2 - 1)

    def col_copy(slot, to_c, to_g, index):
        return pltpu.make_async_remote_copy(
            src_ref=sent.at[to_c],
            dst_ref=cols.at[slot],
            send_sem=col_send.at[index],
            recv_sem=col_recv.at[slot],
            device_id={"chan": to_c, "tgrp": to_g, "pol": me_p},
            device_id_type=MESH,
        )

    def row_copy(slot, to_c, to_g, index):
        return pltpu.make_async_remote_copy(
            src_ref=sent.at[to_c],
            dst_ref=rows.at[slot],
            send_sem=row_send.at[index],
            recv_sem=row_recv.at[slot],
            device_id={"chan": to_c, "tgrp": to_g, "pol": 1 - me_p},
            device_id_type=MESH,
        )

    def each_send(act):
        for place in range(chans):
            to_c = jnp.where(me_c < chans // 2, chans - 1 - place, place)
            for dg in reversed(range(groups)):
                to_g = lax.rem(me_g + dg, groups)
                copy = col_copy(me_f, to_c, to_g, place * groups + dg)
                if dg:
                    act(copy)
                else:
                    pl.when(to_c != me_c)(functools.partial(act, copy))
            for member in range(per_half):
                act(row_copy(me_f, to_c, me_p * per_half + member, place * per_half + member))

    each_send(lambda copy: copy.start())
    cols[me_f] = sent[me_c]

    for dc in range(chans):
        for dg in range(groups):
            if dc or dg:
                from_c, from_g = lax.rem(me_c + dc, chans), lax.rem(me_g + dg, groups)
                col_copy(from_c * groups + from_g, me_c, me_g, 0).wait_recv()
    def put_rows(summed):
        rows_out[0] = summed[: matrix.shape[0]]
        rows_out[1] = summed[matrix.shape[0] :]

    @pl.when(my_half == me_p)
    def _():
        summed = tap_summed(both, cols[...])
        cols_out[...] = summed[: matrix.shape[0]]
        put_rows(summed)

    @pl.when(my_half != me_p)
    def _():
        cols_out[...] = tap_summed(matrix, cols[...])
        for source in range(frames):
            row_copy(source, me_c, me_g, 0).wait_recv()
        put_rows(tap_summed(both, rows[...]))

    each_send(lambda copy: copy.wait_send())


def body(voltages, filter_taps):
    chans, groups = lax.axis_size("chan"), lax.axis_size("tgrp")
    _, length, half = voltages.shape
    taps = filter_taps.shape[0]
    frames = chans * groups
    slot = taps * 2 * CH_DEV
    table = jnp.asarray(twiddle_table(length, chans))
    vmem = pl.BlockSpec(memory_space=pltpu.VMEM)
    summed = CH_DEV * 2 * frames
    row_side, col_side = pl.pallas_call(
        functools.partial(exchange_kernel, chans, groups),
        out_shape=(
            pltpu.VMEM((2, summed, half), jnp.bfloat16),
            pltpu.VMEM((summed, half), jnp.bfloat16),
        ),
        in_specs=[pl.BlockSpec(memory_space=pl.ANY)] * 3,
        out_specs=(vmem, vmem),
        scratch_shapes=[
            pltpu.VMEM((length, half), jnp.bfloat16),
            pltpu.VMEM(filter_taps.shape, jnp.float32),
            pltpu.VMEM(table.shape, jnp.float32),
            pltpu.VMEM((chans, slot, half), LINK),
            pltpu.VMEM((frames, slot, half), LINK),
            pltpu.VMEM((frames, slot, half), LINK),
            pltpu.SemaphoreType.DMA((2 + CHUNKS,)),
            pltpu.SemaphoreType.DMA((frames,)),
            pltpu.SemaphoreType.DMA((frames // 2,)),
            pltpu.SemaphoreType.DMA((frames,)),
            pltpu.SemaphoreType.DMA((frames,)),
        ],
        compiler_params=pltpu.CompilerParams(collective_id=0, has_side_effects=True, vmem_limit_bytes=VMEM_BYTES - SPARE_BYTES - 6 * summed * half),
        name="exchange",
    )(voltages, filter_taps, table)
    rows = half * lax.axis_size("pol") // groups
    tiles = half // 128
    powers = pl.pallas_call(
        functools.partial(power_kernel, frames),
        out_shape=jax.ShapeDtypeStruct((rows * CH_DEV * tiles * 2, 128), jnp.float32),
        in_specs=[vmem, vmem],
        out_specs=pl.BlockSpec(memory_space=pltpu.HBM),
        scratch_shapes=[
            pltpu.VMEM((rows * CH_DEV * tiles * 2, 128), jnp.float32),
            pltpu.VMEM((half, half) if rows != half else (8, 128), jnp.float32),
            pltpu.SemaphoreType.DMA((max(1, rows // 64),)),
        ],
        compiler_params=pltpu.CompilerParams(vmem_limit_bytes=VMEM_BYTES // 4),
        name="powers",
    )(row_side, col_side)
    powers = powers.reshape(rows, CH_DEV, tiles, 2, 128).transpose(0, 1, 3, 2, 4)
    return powers.reshape(rows, CH_DEV, 2, half)


def solution(mesh):
    return jax.shard_map(
        body,
        mesh=mesh,
        in_specs=(P(("beam", "chan", "tgrp"), None, "pol"), P()),
        out_specs=P("tgrp", ("beam", "chan"), None, "pol"),
        check_vma=False,
    )
```
